32 devices in a mesh: groups: 2 (over y), wide: 4 (over z), narrow: 4 (over x, core).
Axes of the slice: x: 2, y: 2, z: 4, core: 2. Of those that a mesh axis runs over, the one named last changes fastest.
Arguments:
- operators: float32 [32, 1024, 1024], P(('groups', 'wide', 'narrow')), parts along dimension 0
- coarse_inverse: float32 [2048, 1024], P(('groups', 'wide'), 'narrow'), parts along dimension 0
- modes: float32 [32, 64, 1024], P(('groups', 'wide', 'narrow')), parts along dimension 0, may hold values from -0.1875 to 0.1875
- gap: float32 [32, 1024, 128], P(('groups', 'wide', 'narrow')), parts along dimension 0, may hold values from -6 to 6
- start_mult: float32 [32, 1024, 128], P(('groups', 'wide', 'narrow')), parts along dimension 0, may hold values from -3 to 3
- peer_list: int32 [32, 256, 1], P(('groups', 'wide', 'narrow')), parts along dimension 0, may hold values from 0 to 3; in each aligned block of 256 rows (0 to 255, 256 to 511, ..., all dimensions but the last counted through in order) at most 128 rows name the same one
- partner_row: int32 [32, 256], P(('groups', 'wide', 'narrow')), parts along dimension 0, may hold values from 0 to 255
- interface_size: int32 [32], P(('groups', 'wide', 'narrow')), parts along dimension 0, may hold values from 512 to 1024, as said below
- contact_rows: int32 [32, 1024], P(('groups', 'wide', 'narrow')), parts along dimension 0, may hold values 0 or 1
Outputs:
- mult: float32 [32, 1024, 128], P(('groups', 'wide', 'narrow')), parts along dimension 0
- residual: float32 [32, 1024, 128], P(('groups', 'wide', 'narrow')), parts along dimension 0
The draws below stay inside these ranges and needn't reach their ends.
There are 2 independent parts, one for each index of `groups`. The reference program is written for one: setup_inputs(seed, part) draws one part's arguments, and reference() takes and returns one part's arrays. A program takes and returns all parts, laid end to end along the dimension named above; each array names one. Nothing has to cross between parts.
Inputs may be any that keep to these rules, and one draw needn't show every extreme that they name: `peer_list`: among the 256 shared rows of one subdomain at most 128 name the same neighbour, and exactly 128 do in some subdomain. `interface_size`: some subdomain has all 1024 rows live.
All inputs are finite; a program needn't handle non-finite values. No bound on the sum of `contact_rows` on one device may be relied on, other than what follows from the above.
Results may differ from the reference program's by a relative error of at most 0.0002.
Values sent between devices are 32-bit elements; how exact they have to be, the bound alone decides.
A program may use at most 64 MiB of HBM per device.

```python
import math
import jax
import jax.numpy as jnp
import numpy as np
from jax import lax

M = 1024
SHARED = 256
MODES = 64
LOADS = 128
OUTER = 2
INNER = 3
WIDE_SUBS = 4
NARROW_SUBS = 4
SUBS = 16
CAP = 128


def draw_operators(key, part):
    first, second = jax.random.split(jax.random.fold_in(key, 11), 2)
    subs = WIDE_SUBS * NARROW_SUBS
    diag = jax.random.uniform(first, (subs, M), jnp.float32, 1.0, 3.0)
    noise = jax.random.normal(second, (subs, M, M), jnp.float32)
    sym = (noise + jnp.swapaxes(noise, 1, 2)) * (0.42 / math.sqrt(M))
    ident = jnp.eye(M, dtype=jnp.float32)
    return sym + ident[None, :, :] * diag[:, :, None]


def draw_coarse_inverse(key, part):
    first, second = jax.random.split(jax.random.fold_in(key, 23), 2)
    size = MODES * WIDE_SUBS * NARROW_SUBS
    rows = jnp.arange(size, dtype=jnp.int32)
    wide_of = rows // (NARROW_SUBS * MODES)
    narrow_of = rows // MODES % NARROW_SUBS
    matched = (narrow_of * WIDE_SUBS + wide_of) * MODES + rows % MODES
    base = (rows[None, :] == matched[:, None]).astype(jnp.float32)
    scales = jax.random.uniform(first, (size, 1), jnp.float32, 0.5, 1.5)
    noise = jax.random.normal(second, (size, size), jnp.float32) * (0.5 / math.sqrt(size))
    return base * scales + noise


def draw_interface_size(key, part):
    first, second = jax.random.split(jax.random.fold_in(key, 37), 2)
    subs = WIDE_SUBS * NARROW_SUBS
    sizes = jax.random.randint(first, (subs,), M // 2, M + 1, dtype=jnp.int32)
    spot = jax.random.randint(second, (), 0, subs, dtype=jnp.int32)
    return jnp.where(jnp.arange(subs, dtype=jnp.int32) == spot, M, sizes).astype(jnp.int32)


def set_ends(entries, rng, smallest, largest):
    place = [jax.random.randint(jax.random.fold_in(rng, axis), (), 0, length) for axis, length in enumerate(entries.shape)]
    widest = entries.shape.index(max(entries.shape))
    neighbour = place[:widest] + [(place[widest] + 1) % entries.shape[widest]] + place[widest + 1:]
    return entries.at[tuple(place)].set(smallest).at[tuple(neighbour)].set(largest)


def level_of(rng, shape, cuts, smallest, largest):
    loudness = 1.0
    for axis_at, shards_of in cuts:
        draws = jax.random.uniform(jax.random.fold_in(jax.random.fold_in(rng, 6), axis_at), (shards_of,), jnp.float32, smallest / len(cuts), largest / len(cuts))
        loudness = loudness * jnp.repeat(jnp.exp(draws), shape[axis_at] // shards_of).reshape((-1,) + (1,) * (len(shape) - 1 - axis_at))
    return loudness


def shared_out(rng, own, number, rows, number_of, top, reach, skew):
    order = jax.random.permutation(rng, number_of)
    heavy_load, ordinary = portions_of(number_of, rows * top, reach, skew, True), portions_of(number_of, rows * top, reach, skew, False)
    places = jnp.arange(number_of)

    def named(lengths, rotation):
        used = int((lengths > 0).sum())
        fixed = max(1, used // 4)
        passed = fixed + (places - fixed + rotation * (used - fixed)) % max(1, number_of - fixed)
        return jnp.zeros((number_of,), jnp.int32).at[order[jnp.where(places < fixed, places, passed)]].set(jnp.asarray(lengths, jnp.int32))

    lengths = jnp.where(number % 4 == 0, named(heavy_load, number // 4), named(ordinary, number - number // 4 - 1))
    mixed = jax.random.permutation(jax.random.fold_in(own, 3), number_of)
    donor, receiver = mixed[0:number_of // 2 * 2:2], mixed[1:number_of // 2 * 2:2]
    slack = jnp.minimum(lengths[donor] - 1, reach - lengths[receiver]) // 2
    slack = jnp.where((donor == order[0]) | (receiver == order[0]) | (lengths[receiver] == 0), 0, jnp.maximum(slack, 0))
    passed = jax.random.randint(jax.random.fold_in(own, 4), (number_of // 2,), 0, 1 << 20) % (slack + 1)
    lengths = lengths.at[donor].add(-passed).at[receiver].add(passed)
    items = jnp.searchsorted(jnp.cumsum(lengths), jnp.arange(rows * top), side="right").astype(jnp.int32)
    grid = items.reshape(top, rows).T
    grid = grid[jax.random.permutation(jax.random.fold_in(own, 1), rows)]
    rotation = jax.random.randint(jax.random.fold_in(own, 2), (rows, 1), 0, top)
    return jnp.take_along_axis(grid, (jnp.arange(top)[None, :] + rotation) % top, axis=1)


def portions_of(count, total, most, lean, full):
    portions = [(1 << 20) // math.isqrt(rank ** lean) + 1 for rank in range(1, count + 1)]
    largest = most if full else min(most, max(-(-total // count), total * portions[0] // sum(portions)))
    least = 1 if total - largest >= count - 1 else 0
    counts, rest = [largest] + [least] * (count - 1), total - largest - least * (count - 1)
    while rest > 0:
        candidates = [i for i in range(1, count) if counts[i] < largest] or [i for i in range(1, count) if counts[i] < most]
        mass, left = sum([portions[i] for i in candidates]), rest
        for i in candidates:
            extra = min(most - counts[i], max(1, left * portions[i] // mass), rest)
            counts[i] = counts[i] + extra
            rest = rest - extra
    return np.array(counts)


def gaussian(own_key, extent, scale, limit, shards=(), held_as=jnp.bfloat16):
    entries = scale * jax.random.normal(own_key, extent, jnp.float32)
    if shards:
        entries = entries * level_of(own_key, extent, shards, -0.22, 0.18)
    return jnp.clip(entries, -limit, limit).astype(held_as)


def setup_inputs(seed: int = 0, part: int = 0) -> dict:
    key_of = jax.random.split(jax.random.key(seed), 10)
    part_keys = jax.random.split(jax.random.fold_in(key_of[9], part), 10)
    operators = draw_operators(jax.random.fold_in(jax.random.fold_in(key_of[9], part), 71), part)
    coarse_inverse = draw_coarse_inverse(jax.random.fold_in(jax.random.fold_in(key_of[9], part), 71), part)
    modes = gaussian(part_keys[2], (SUBS, MODES, M), M ** -0.5, 0.1875, ((0, 16),), jnp.float32)
    gap = gaussian(part_keys[3], (SUBS, M, LOADS), 1.0, 6.0, ((0, 16),), jnp.float32)
    start_mult = gaussian(part_keys[4], (SUBS, M, LOADS), 0.5, 3.0, ((0, 16),), jnp.float32)
    peer_list_keys = jax.random.split(jax.random.fold_in(part_keys[5], 1), SUBS * SHARED // SHARED)
    peer_list_turns = jax.random.permutation(jax.random.fold_in(part_keys[5], 3), SUBS * SHARED // SHARED)
    peer_list = jax.vmap(lambda own, number: shared_out(jax.random.fold_in(part_keys[5], 2), own, number, SHARED, WIDE_SUBS, 1, CAP, 2))(peer_list_keys, peer_list_turns).reshape((SUBS, SHARED, 1))
    partner_row = set_ends(jax.random.randint(part_keys[6], (SUBS, SHARED), 0, SHARED), jax.random.fold_in(part_keys[6], 1), 0, SHARED - 1).astype(jnp.int32)
    interface_size = draw_interface_size(jax.random.fold_in(jax.random.fold_in(key_of[9], part), 71), part)
    contact_rows = set_ends((jax.random.randint(part_keys[8], (SUBS, M), 0, 2) < 1).astype(jnp.int32), jax.random.fold_in(part_keys[8], 1), 0, 1)
    return {"operators": operators, "coarse_inverse": coarse_inverse, "modes": modes, "gap": gap, "start_mult": start_mult, "peer_list": peer_list, "partner_row": partner_row, "interface_size": interface_size, "contact_rows": contact_rows}


def reference(operators, coarse_inverse, modes, gap, start_mult, peer_list, partner_row, interface_size, contact_rows):
    subs = WIDE_SUBS * NARROW_SUBS
    highest = lax.Precision.HIGHEST
    active = (jnp.arange(M, dtype=jnp.int32)[None, :] < interface_size[:, None])[:, :, None]
    contact = (contact_rows == 1)[:, :, None]
    owner = peer_list[:, :, 0] * NARROW_SUBS + (jnp.arange(subs, dtype=jnp.int32) % NARROW_SUBS)[:, None]
    flat_index = (owner * M + partner_row).astype(jnp.int32)
    mult = start_mult
    residual = jnp.zeros_like(gap)
    for outer in range(OUTER):
        for inner in range(INNER):
            image = jnp.einsum("smn,snk->smk", operators, mult, precision=highest)
            across = image.reshape(subs * M, LOADS)[flat_index]
            jump = jnp.concatenate([image[:, :SHARED] - across, image[:, SHARED:]], axis=1)
            residual = jnp.where(active, gap - jump, 0.0)
            update = 0.3 * residual
            if inner == 0:
                coarse = jnp.einsum("scm,smk->sck", modes, residual, precision=highest)
                ordered = coarse.reshape(WIDE_SUBS, NARROW_SUBS, MODES, LOADS).transpose(1, 0, 2, 3).reshape(subs * MODES, LOADS)
                solved = jnp.dot(coarse_inverse, ordered, precision=highest, preferred_element_type=jnp.float32).reshape(subs, MODES, LOADS)
                update = update + jnp.einsum("scm,sck->smk", modes, solved, precision=highest)
            trial = mult + update
            mult = jnp.where(active, jnp.where(contact, jnp.maximum(trial, 0.0), trial), 0.0)
    return mult, residual
```

```python
import functools

import jax
import jax.numpy as jnp
from jax import lax
from jax.experimental import pallas as pl
from jax.experimental.pallas import tpu as pltpu
from jax.sharding import PartitionSpec as P

OUTER = 2
INNER = 3
F32 = jnp.float32
BF16 = jnp.bfloat16
MESH = pl.DeviceIdType.MESH


def kernel(
    wides,
    narrows,
    operator_hbm,
    inverse_hbm,
    modes_hbm,
    gap_hbm,
    start_hbm,
    peers_hbm,
    partner_hbm,
    size_ref,
    contact_hbm,
    mult_out,
    res_out,
    op_f32,
    op_hi,
    op_lo,
    inv_f32,
    inv_hl,
    modes_f32,
    modes_hl,
    modes_t,
    gap_f32,
    start_f32,
    gap_d,
    floor_d,
    mult_d,
    res_d,
    mix_d,
    choose,
    scatter,
    idx_out,
    idx_in,
    pack,
    land,
    coarse_all,
    part,
    solved_in,
    peers_ref,
    partner_ref,
    contact_ref,
    pre_top,
    load_sem,
    idx_send,
    idx_recv,
    x_send,
    x_recv,
    c_send,
    c_recv,
    n_send,
    n_recv,
):
    order, loads = gap_f32.shape
    shared = peers_ref.shape[1]
    modes = modes_f32.shape[0]
    half = loads // 2
    slots = scatter.shape[1]
    cap = slots // wides
    blocks = order // shared
    w = lax.axis_index("wide")
    n = lax.axis_index("narrow")

    def load(src, dst, k):
        return pltpu.make_async_copy(src, dst, load_sem.at[k])

    small = [
        load(peers_hbm, peers_ref, 4 + blocks),
        load(partner_hbm, partner_ref, 5 + blocks),
        load(contact_hbm, contact_ref, 6 + blocks),
    ]
    for copy in small:
        copy.start()
    loads_of = [load(start_hbm, start_f32, 0)]
    for b in range(blocks):
        rows = pl.ds(b * shared, shared)
        loads_of.append(load(operator_hbm.at[rows], op_f32.at[rows], 1 + b))
    loads_of.append(load(gap_hbm, gap_f32, 1 + blocks))
    loads_of.append(load(modes_hbm, modes_f32, 2 + blocks))
    loads_of.append(load(inverse_hbm, inv_f32, 3 + blocks))
    for copy in loads_of:
        copy.start()

    barrier = pltpu.get_barrier_semaphore()
    for d in range(1, wides):
        pl.semaphore_signal(
            barrier, inc=1, device_id={"wide": lax.rem(w + d, wides)}, device_id_type=MESH
        )
    for d in range(1, narrows):
        pl.semaphore_signal(
            barrier, inc=1, device_id={"narrow": lax.rem(n + d, narrows)}, device_id_type=MESH
        )

    for copy in small:
        copy.wait()
    peer_row = peers_ref[...].astype(F32)
    peer_col = jnp.broadcast_to(peer_row, (loads, shared)).T[:, :1]
    before = lax.broadcasted_iota(jnp.int32, (shared, shared), 1) < lax.broadcasted_iota(
        jnp.int32, (shared, shared), 0
    )
    same = jnp.broadcast_to(peer_row, (shared, shared)) == peer_col
    rank = jnp.sum(jnp.where(before & same, 1.0, 0.0), axis=1, keepdims=True)
    ahead = peer_col - w.astype(F32)
    ahead = jnp.where(ahead < 0.0, ahead + float(wides), ahead)
    target = jnp.broadcast_to(ahead * float(cap) + rank, (shared, slots))
    column = lax.broadcasted_iota(jnp.int32, (shared, slots), 1).astype(F32)
    partner_col = jnp.broadcast_to(partner_ref[...].astype(F32), (loads, shared)).T[:, :1]
    wanted = jnp.sum(
        jnp.where(target == column, jnp.broadcast_to(partner_col, (shared, slots)), 0.0),
        axis=0,
        keepdims=True,
    )
    for d in range(wides):
        idx_out[d] = jnp.broadcast_to(wanted[:, d * cap : (d + 1) * cap], idx_out.shape[1:])
    pl.semaphore_wait(barrier, wides - 1 + narrows - 1)
    idx_copies = []
    for d in range(1, wides):
        copy = pltpu.make_async_remote_copy(
            src_ref=idx_out.at[d],
            dst_ref=idx_in.at[d],
            send_sem=idx_send.at[d],
            recv_sem=idx_recv.at[d],
            device_id={"wide": lax.rem(w + d, wides)},
            device_id_type=MESH,
        )
        copy.start()
        idx_copies.append(copy)
    scatter[...] = jnp.where(target == column, 1.0, 0.0).astype(BF16)

    def low(shape):
        return lax.broadcasted_iota(jnp.int32, shape, 1) < half

    def mix(x):
        return jnp.where(low(x.shape), x, x - x.astype(BF16).astype(F32)).astype(BF16)

    def turn(x):
        return pltpu.roll(x, half, 1)

    def fold(x):
        return x + turn(x)

    def dup(x):
        y = turn(x)
        m = low(x.shape)
        return jnp.where(m, x, y), jnp.where(m, y, x)

    def mat(a, b):
        return jnp.dot(a, b, preferred_element_type=F32)

    def side(h):
        return slice(h * loads, (h + 1) * loads)

    loads_of[0].wait()
    for h, x in enumerate(dup(start_f32[...])):
        mult_d[h] = x
        mix_d[:, side(h)] = mix(x)

    steps = OUTER * INNER

    def split_rows(b):
        loads_of[1 + b].wait()
        x = op_f32[pl.ds(b * shared, shared), :]
        hi = x.astype(BF16)
        op_hi[pl.ds(b * shared, shared), :] = hi
        op_lo[pl.ds(b * shared, shared), :] = (x - hi.astype(F32)).astype(BF16)

    def active(b):
        return (
            b * shared + lax.broadcasted_iota(jnp.int32, (shared, loads), 0)
        ) < size_ref[0]

    image_top = [None, None]
    pre_coarse = [None, None]

    def top_of(h, first, last):
        rhs = mix_d[first:last, side(h)]
        return mat(op_hi[:shared, first:last], rhs) + mat(op_lo[:shared, first:last], rhs)

    def exchange(t, h, d):
        return pltpu.make_async_remote_copy(
            src_ref=pack.at[t % 2, h, d],
            dst_ref=land.at[t % 2, h, d],
            send_sem=x_send.at[t % 2, h, d],
            recv_sem=x_recv.at[t % 2, h, d],
            device_id={"wide": lax.rem(w + wides - d, wides)},
            device_id_type=MESH,
        )

    far = sorted(range(1, wides), key=lambda d: -min(d, wides - d))

    def send(t, h):
        if t == 0:
            image_top[h] = pre_top[h]
        elif t % INNER == 1:
            image_top[h] = fold(top_of(h, 0, order))
        else:
            image_top[h] = fold(pre_top[h] + top_of(h, 0, shared))
        if t >= 2:
            for d in range(1, wides):
                exchange(t, h, d).wait_send()
        first = low((cap // 2, loads))
        picked = mix(image_top[h])
        chosen = fold(mat(choose[...], picked))
        for d in far + [0]:
            value = jnp.where(
                first,
                chosen[d * cap : d * cap + cap // 2],
                chosen[d * cap + cap // 2 : (d + 1) * cap],
            )
            if d == 0:
                land[t % 2, h, 0] = value
            else:
                pack[t % 2, h, d] = value
                exchange(t, h, d).start()

    def advance(b, h, update):
        rows = pl.ds(pl.multiple_of(b * shared, shared), shared)
        trial = jnp.maximum(mult_d[h, rows, :] + update, floor_d[rows, :])
        new = jnp.where(active(b), trial, 0.0)
        mult_d[h, rows, :] = new
        mix_d[rows, side(h)] = mix(new)

    def bottom(t):
        @pl.loop(1, blocks)
        def _(b):
            rows = pl.ds(pl.multiple_of(b * shared, shared), shared)
            rhs = mix_d[...]
            image = mat(op_hi[rows, :], rhs) + mat(op_lo[rows, :], rhs)
            for h in range(2):
                res_d[h, rows, :] = jnp.where(
                    active(b), gap_d[h, rows, :] - fold(image[:, side(h)]), 0.0
                )

        if t % INNER:

            @pl.loop(1, blocks)
            def _(b):
                rows = pl.ds(pl.multiple_of(b * shared, shared), shared)
                for h in range(2):
                    advance(b, h, 0.3 * res_d[h, rows, :])

            if t + 1 < steps:
                rhs = mix_d[shared:, :]
                pre = mat(op_hi[:shared, shared:], rhs) + mat(op_lo[:shared, shared:], rhs)
                for h in range(2):
                    pre_top[h] = pre[:, side(h)]
        else:
            rhs = jnp.concatenate([mix(res_d[h, shared:, :]) for h in range(2)], axis=1)
            pre = mat(modes_hl[:, shared:], rhs)
            for h in range(2):
                pre_coarse[h] = pre[:, side(h)]

    def receive(t, h):
        for d in range(1, wides):
            exchange(t, h, d).wait_recv()
        pieces = []
        for d in range(wides):
            pieces.extend(dup(land[t % 2, h, d]))
        rhs = mix(jnp.concatenate(pieces, axis=0))
        across = mat(scatter[...], rhs)
        across = fold(across)
        res = jnp.where(active(0), gap_d[h, :shared, :] - (image_top[h] - across), 0.0)
        res_d[h, :shared, :] = res
        if t % INNER:
            advance(0, h, 0.3 * res)

    def coarse_copy(o, h, d):
        return pltpu.make_async_remote_copy(
            src_ref=coarse_all.at[o, h, w],
            dst_ref=coarse_all.at[o, h, w],
            send_sem=c_send.at[o, h, d],
            recv_sem=c_recv.at[o, h, d],
            device_id={"wide": lax.rem(w + wides - d, wides)},
            device_id_type=MESH,
        )

    def coarse_send(t, h):
        o = t // INNER
        both = pre_coarse[h] + mat(modes_hl[:, :shared], mix(res_d[h, :shared, :]))
        c = fold(both[:modes] + both[modes:])
        coarse_all[o, h, w] = jnp.where(
            low((modes // 2, loads)), c[: modes // 2], c[modes // 2 :]
        )
        for d in far:
            coarse_copy(o, h, d).start()

    def solved_copy(o, h, d):
        return pltpu.make_async_remote_copy(
            src_ref=part.at[o, h, lax.rem(n + d, narrows)],
            dst_ref=solved_in.at[o, h, d],
            send_sem=n_send.at[o, h, d],
            recv_sem=n_recv.at[o, h, d],
            device_id={"narrow": lax.rem(n + d, narrows)},
            device_id_type=MESH,
        )

    def coarse_mid(t, h):
        o = t // INNER
        for d in range(1, wides):
            coarse_copy(o, h, d).wait_recv()
        pieces = []
        for k in range(wides):
            pieces.extend(dup(coarse_all[o, h, k]))
        both = mat(inv_hl[...], mix(jnp.concatenate(pieces, axis=0)))
        size = narrows * modes
        p = fold(both[:size] + both[size:])
        first = low((modes // 2, loads))
        for k in range(narrows):
            part[o, h, k] = jnp.where(
                first,
                p[k * modes : k * modes + modes // 2],
                p[k * modes + modes // 2 : (k + 1) * modes],
            )
        for d in range(1, narrows):
            solved_copy(o, h, d).start()

    def coarse_end(t, h):
        o = t // INNER
        total = part[o, h, n]
        for d in range(1, narrows):
            solved_copy(o, h, d).wait_recv()
            total = total + solved_in[o, h, d]
        s = mix(jnp.concatenate(dup(total), axis=0))
        s = jnp.concatenate([s, s], axis=0)

        for b in range(blocks):
            rows = pl.ds(b * shared, shared)
            advance(b, h, 0.3 * res_d[h, rows, :] + fold(mat(modes_t[rows, :], s)))

    split_rows(0)
    for h in range(2):
        pre_top[h] = fold(top_of(h, 0, order))
    for b in range(1, blocks):
        split_rows(b)
    loads_of[1 + blocks].wait()
    for h, x in enumerate(dup(gap_f32[...])):
        gap_d[h] = x
    wall = jnp.where(contact_ref[...] == 1, 0.0, -jnp.inf)
    floor_d[...] = jnp.broadcast_to(wall, (loads, order)).T
    loads_of[2 + blocks].wait()
    m = modes_f32[...]
    m_hi = m.astype(BF16).astype(F32)
    modes_hl[:modes, :] = m.astype(BF16)
    modes_hl[modes:, :] = (m - m_hi).astype(BF16)
    modes_t[...] = jnp.concatenate([m_hi, m - m_hi], axis=0).T.astype(BF16)
    pieces = [wanted[:, :cap]]
    for d in range(1, wides):
        idx_copies[d - 1].wait_recv()
        pieces.append(idx_in[d, 0:1, :])
    index = jnp.concatenate(pieces, axis=1)
    rowid = lax.broadcasted_iota(jnp.int32, (shared, slots), 0).astype(F32)
    choose[...] = (
        jnp.where(rowid == jnp.broadcast_to(index, (shared, slots)), 1.0, 0.0).T.astype(BF16)
    )

    send(0, 0)
    send(0, 1)
    bottom(0)
    loads_of[3 + blocks].wait()
    inv = inv_f32[...]
    inv_hi = inv.astype(BF16)
    size = narrows * modes
    inv_hl[:size, :] = inv_hi
    inv_hl[size:, :] = (inv - inv_hi.astype(F32)).astype(BF16)

    def emit(rows):
        first = low((rows.stop - rows.start, loads))
        mult_out[rows, :] = jnp.where(first, mult_d[0, rows, :], mult_d[1, rows, :])
        res_out[rows, :] = jnp.where(first, res_d[0, rows, :], res_d[1, rows, :])

    for t in range(steps):
        if t + 1 == steps and t % INNER:
            emit(slice(shared, order))
        if t % INNER == 0:
            for h in range(2):
                receive(t, h)
                coarse_send(t, h)
            for h in range(2):
                coarse_mid(t, h)
            for h in range(2):
                coarse_end(t, h)
                if t + 1 < steps:
                    send(t + 1, h)
            if t + 1 < steps:
                bottom(t + 1)
        else:
            for h in range(2):
                receive(t, h)
                if t + 1 < steps:
                    send(t + 1, h)
            if t + 1 < steps:
                bottom(t + 1)

    emit(slice(0, shared))
    for copy in idx_copies:
        copy.wait_send()
    for t in range(max(0, steps - 2), steps):
        for h in range(2):
            for d in range(1, wides):
                exchange(t, h, d).wait_send()
    for o in range(OUTER):
        for h in range(2):
            for d in range(1, wides):
                coarse_copy(o, h, d).wait_send()
            for d in range(1, narrows):
                solved_copy(o, h, d).wait_send()


def flush(mult, residual, mult_hbm, residual_hbm, sem):
    copies = [
        pltpu.make_async_copy(mult, mult_hbm, sem.at[0]),
        pltpu.make_async_copy(residual, residual_hbm, sem.at[1]),
    ]
    for copy in copies:
        copy.start()
    for copy in copies:
        copy.wait()


def local(
    wides,
    narrows,
    operators,
    coarse_inverse,
    modes,
    gap,
    start_mult,
    peer_list,
    partner_row,
    interface_size,
    contact_rows,
):
    order, loads = gap.shape[1:]
    shared = partner_row.shape[1]
    count = modes.shape[1]
    slots = 2 * shared
    cap = slots // wides
    far = pl.BlockSpec(memory_space=pltpu.HBM)
    near = pl.BlockSpec(memory_space=pltpu.VMEM)
    out = jax.ShapeDtypeStruct((order, loads), F32)
    held = pltpu.VMEM((order, loads), F32)
    dma = pltpu.SemaphoreType.DMA
    mult, residual = pl.pallas_call(
        functools.partial(kernel, wides, narrows),
        out_shape=(held, held),
        in_specs=[far] * 7 + [pl.BlockSpec(memory_space=pltpu.SMEM), far],
        out_specs=(near, near),
        scratch_shapes=[
            pltpu.VMEM((order, order), F32),
            pltpu.VMEM((order, order), BF16),
            pltpu.VMEM((order, order), BF16),
            pltpu.VMEM(coarse_inverse.shape, F32),
            pltpu.VMEM((2 * coarse_inverse.shape[0], coarse_inverse.shape[1]), BF16),
            pltpu.VMEM((count, order), F32),
            pltpu.VMEM((2 * count, order), BF16),
            pltpu.VMEM((order, 2 * count), BF16),
            pltpu.VMEM((order, loads), F32),
            pltpu.VMEM((order, loads), F32),
            pltpu.VMEM((2, order, loads), F32),
            pltpu.VMEM((order, loads), F32),
            pltpu.VMEM((2, order, loads), F32),
            pltpu.VMEM((2, order, loads), F32),
            pltpu.VMEM((order, 2 * loads), BF16),
            pltpu.VMEM((slots, shared), BF16),
            pltpu.VMEM((shared, slots), BF16),
            pltpu.VMEM((wides, 8, cap), F32),
            pltpu.VMEM((wides, 8, cap), F32),
            pltpu.VMEM((2, 2, wides, cap // 2, loads), F32),
            pltpu.VMEM((2, 2, wides, cap // 2, loads), F32),
            pltpu.VMEM((OUTER, 2, wides, count // 2, loads), F32),
            pltpu.VMEM((OUTER, 2, narrows, count // 2, loads), F32),
            pltpu.VMEM((OUTER, 2, narrows, count // 2, loads), F32),
            pltpu.VMEM((1, shared), jnp.int32),
            pltpu.VMEM((1, shared), jnp.int32),
            pltpu.VMEM((1, order), jnp.int32),
            pltpu.VMEM((2, shared, loads), F32),
            dma((7 + order // shared,)),
            dma((wides,)),
            dma((wides,)),
            dma((2, 2, wides)),
            dma((2, 2, wides)),
            dma((OUTER, 2, wides)),
            dma((OUTER, 2, wides)),
            dma((OUTER, 2, narrows)),
            dma((OUTER, 2, narrows)),
        ],
        compiler_params=pltpu.CompilerParams(
            collective_id=0, has_side_effects=True, vmem_limit_bytes=67043328 - 2 * order * loads * 4
        ),
        name="feti",
    )(
        operators[0],
        coarse_inverse,
        modes[0],
        gap[0],
        start_mult[0],
        peer_list.reshape(1, shared),
        partner_row,
        interface_size,
        contact_rows,
    )
    mult, residual = pl.pallas_call(
        flush,
        out_shape=(out, out),
        in_specs=[near] * 2,
        out_specs=(far, far),
        scratch_shapes=[dma((2,))],
        compiler_params=pltpu.CompilerParams(vmem_limit_bytes=2**20),
        name="flush",
    )(mult, residual)
    return (mult[None], residual[None])


def solution(mesh):
    everyone = ("groups", "wide", "narrow")
    return jax.shard_map(
        functools.partial(local, mesh.shape["wide"], mesh.shape["narrow"]),
        mesh=mesh,
        in_specs=(
            P(everyone, None, None),
            P(("groups", "wide"), "narrow"),
            P(everyone, None, None),
            P(everyone, None, None),
            P(everyone, None, None),
            P(everyone, None, None),
            P(everyone, None),
            P(everyone),
            P(everyone, None),
        ),
        out_specs=(P(everyone, None, None), P(everyone, None, None)),
        check_vma=False,
    )
```

```python
import functools

import jax
import jax.numpy as jnp
from jax import lax
from jax.experimental import pallas as pl
from jax.experimental.pallas import tpu as pltpu
from jax.sharding import PartitionSpec as P

OUTER = 2
INNER = 3
F32 = jnp.float32
BF16 = jnp.bfloat16
MESH = pl.DeviceIdType.MESH


def kernel(
    wides,
    narrows,
    operator_hbm,
    inverse_hbm,
    modes_hbm,
    gap_hbm,
    start_hbm,
    peers_hbm,
    partner_hbm,
    size_ref,
    contact_hbm,
    mult_out,
    res_out,
    op_f32,
    op_hi,
    op_lo,
    inv_f32,
    inv_hl,
    modes_f32,
    modes_hl,
    modes_t,
    gap_f32,
    start_f32,
    gap_d,
    floor_d,
    mult_d,
    res_d,
    mix_d,
    choose,
    scatter,
    idx_out,
    idx_in,
    pack,
    land,
    coarse_all,
    part,
    solved_in,
    peers_ref,
    partner_ref,
    contact_ref,
    pre_top,
    pre_sel,
    pre_coarse,
    sel_hi,
    sel_lo,
    modes_s,
    load_sem,
    idx_send,
    idx_recv,
    x_send,
    x_recv,
    c_send,
    c_recv,
    n_send,
    n_recv,
):
    order, loads = gap_f32.shape
    shared = peers_ref.shape[1]
    modes = modes_f32.shape[0]
    half = loads // 2
    slots = scatter.shape[1]
    cap = slots // wides
    blocks = order // shared
    w = lax.axis_index("wide")
    n = lax.axis_index("narrow")

    barrier = pltpu.get_barrier_semaphore()
    for d in range(1, wides):
        pl.semaphore_signal(
            barrier, inc=1, device_id={"wide": lax.rem(w + d, wides)}, device_id_type=MESH
        )
    for d in range(1, narrows):
        pl.semaphore_signal(
            barrier, inc=1, device_id={"narrow": lax.rem(n + d, narrows)}, device_id_type=MESH
        )

    def load(src, dst, k):
        return pltpu.make_async_copy(src, dst, load_sem.at[k])

    small = [
        load(peers_hbm, peers_ref, 4 + blocks),
        load(partner_hbm, partner_ref, 5 + blocks),
        load(contact_hbm, contact_ref, 6 + blocks),
    ]
    for copy in small:
        copy.start()
    loads_of = [load(start_hbm, start_f32, 0)]
    for b in range(blocks):
        rows = pl.ds(b * shared, shared)
        loads_of.append(load(operator_hbm.at[rows], op_f32.at[rows], 1 + b))
    loads_of.append(load(gap_hbm, gap_f32, 1 + blocks))
    loads_of.append(load(modes_hbm, modes_f32, 2 + blocks))
    loads_of.append(load(inverse_hbm, inv_f32, 3 + blocks))
    for copy in loads_of:
        copy.start()

    for copy in small:
        copy.wait()
    peer_row = peers_ref[...].astype(F32)
    peer_col = jnp.broadcast_to(peer_row, (loads, shared)).T[:, :1]
    before = lax.broadcasted_iota(jnp.int32, (shared, shared), 1) < lax.broadcasted_iota(
        jnp.int32, (shared, shared), 0
    )
    same = jnp.broadcast_to(peer_row, (shared, shared)) == peer_col
    rank = jnp.sum(jnp.where(before & same, 1.0, 0.0), axis=1, keepdims=True)
    ahead = peer_col - w.astype(F32)
    ahead = jnp.where(ahead < 0.0, ahead + float(wides), ahead)
    target = jnp.broadcast_to(ahead * float(cap) + rank, (shared, slots))
    column = lax.broadcasted_iota(jnp.int32, (shared, slots), 1).astype(F32)
    partner_col = jnp.broadcast_to(partner_ref[...].astype(F32), (loads, shared)).T[:, :1]
    wanted = jnp.sum(
        jnp.where(target == column, jnp.broadcast_to(partner_col, (shared, slots)), 0.0),
        axis=0,
        keepdims=True,
    )
    for d in range(wides):
        idx_out[d] = jnp.broadcast_to(wanted[:, d * cap : (d + 1) * cap], idx_out.shape[1:])
    pl.semaphore_wait(barrier, wides - 1 + narrows - 1)
    idx_copies = []
    for d in range(1, wides):
        copy = pltpu.make_async_remote_copy(
            src_ref=idx_out.at[d],
            dst_ref=idx_in.at[d],
            send_sem=idx_send.at[d],
            recv_sem=idx_recv.at[d],
            device_id={"wide": lax.rem(w + d, wides)},
            device_id_type=MESH,
        )
        copy.start()
        idx_copies.append(copy)
    live = lax.broadcasted_iota(jnp.int32, (shared, slots), 0) < size_ref[0]
    scatter[...] = jnp.where((target == column) & live, 1.0, 0.0).astype(BF16)

    def low(shape):
        return lax.broadcasted_iota(jnp.int32, shape, 1) < half

    def mix(x):
        return jnp.where(low(x.shape), x, x - x.astype(BF16).astype(F32)).astype(BF16)

    def turn(x):
        return pltpu.roll(x, half, 1)

    def fold(x):
        return x + turn(x)

    def dup(x):
        y = turn(x)
        m = low(x.shape)
        return jnp.where(m, x, y), jnp.where(m, y, x)

    def mat(a, b):
        return jnp.dot(a, b, preferred_element_type=F32)

    def side(h):
        return slice(h * loads, (h + 1) * loads)

    loads_of[0].wait()
    for h, x in enumerate(dup(start_f32[...])):
        mult_d[h] = x
        mix_d[:, side(h)] = mix(x)

    steps = OUTER * INNER

    def split_rows(b):
        loads_of[1 + b].wait()
        x = op_f32[pl.ds(b * shared, shared), :]
        hi = x.astype(BF16)
        op_hi[pl.ds(b * shared, shared), :] = hi
        op_lo[pl.ds(b * shared, shared), :] = (x - hi.astype(F32)).astype(BF16)

    def active(b):
        return (
            b * shared + lax.broadcasted_iota(jnp.int32, (shared, loads), 0)
        ) < size_ref[0]

    def top_of(h, first, last):
        rhs = mix_d[first:last, side(h)]
        return mat(op_hi[:shared, first:last], rhs) + mat(op_lo[:shared, first:last], rhs)

    def exchange(t, h, d):
        slot = lax.rem(t, 2)
        return pltpu.make_async_remote_copy(
            src_ref=pack.at[slot, h, d],
            dst_ref=land.at[slot, h, d],
            send_sem=x_send.at[slot, h, d],
            recv_sem=x_recv.at[slot, h, d],
            device_id={"wide": lax.rem(w + wides - d, wides)},
            device_id_type=MESH,
        )

    def peer(k):
        up = wides - 2 - k + jnp.where(wides - 2 - k >= w, 1, 0)
        down = k + 1 - jnp.where(k + 1 <= w, 1, 0)
        return jnp.where(w < wides // 2, down, up)

    def turn_of(k):
        return lax.rem(w + wides - peer(k), wides)


    def send(t, h, chosen):
        first = low((cap // 2, loads))
        for d in sorted(range(1, wides), key=lambda d: -min(d, wides - d)) + [0]:
            value = jnp.where(
                first,
                chosen[d * cap : d * cap + cap // 2],
                chosen[d * cap + cap // 2 : (d + 1) * cap],
            )
            if d == 0:
                land[lax.rem(t, 2), h, 0] = value
            else:
                pack[lax.rem(t, 2), h, d] = value
                exchange(t, h, d).start()

    def advance(b, h, update):
        rows = pl.ds(b * shared, shared)
        if not isinstance(b, int):
            rows = pl.ds(pl.multiple_of(b * shared, shared), shared)
        trial = jnp.maximum(mult_d[h, rows, :] + update, floor_d[rows, :])
        new = jnp.where(active(b), trial, 0.0)
        mixed = mix(new)
        mult_d[h, rows, :] = new
        mix_d[rows, side(h)] = mixed
        return mixed

    def free(t, h):
        for d in range(1, wides):
            exchange(t, h, d).wait_send()

    def bottom(kind, last):
        @pl.loop(0, blocks)
        def _(b):
            rows = pl.ds(pl.multiple_of(b * shared, shared), shared)
            rhs = mix_d[...]
            image = mat(op_hi[rows, :], rhs) + mat(op_lo[rows, :], rhs)
            for h in range(2):
                res_d[h, rows, :] = jnp.where(
                    active(b), gap_d[h, rows, :] - fold(image[:, side(h)]), 0.0
                )

        if kind == "plain":

            @pl.loop(1, blocks)
            def _(b):
                rows = pl.ds(pl.multiple_of(b * shared, shared), shared)
                for h in range(2):
                    advance(b, h, 0.3 * res_d[h, rows, :])

            @pl.when(jnp.logical_not(last))
            def _():
                rhs = mix_d[shared:, :]
                pre = mat(sel_hi[:, shared:], rhs) + mat(sel_lo[:, shared:], rhs)
                for h in range(2):
                    pre_sel[h] = pre[:, side(h)]
        else:
            rhs = jnp.concatenate([mix(res_d[h]) for h in range(2)], axis=1)
            pre = mat(modes_hl[...], rhs)
            for h in range(2):
                mult_d[h, shared:, :] += 0.3 * res_d[h, shared:, :]
            for h in range(2):
                pre_coarse[h] = pre[:, side(h)]

    def coarse_copy(o, h, d):
        return pltpu.make_async_remote_copy(
            src_ref=coarse_all.at[o, h, w],
            dst_ref=coarse_all.at[o, h, w],
            send_sem=c_send.at[o, h, d],
            recv_sem=c_recv.at[o, h, d],
            device_id={"wide": lax.rem(w + wides - d, wides)},
            device_id_type=MESH,
        )

    def coarse_send(o, h, rhs):
        both = pre_coarse[h] + mat(modes_s[...], rhs)
        c = fold(both[:modes] + both[modes:])
        coarse_all[o, h, w] = jnp.where(
            low((modes // 2, loads)), c[: modes // 2], c[modes // 2 :]
        )
        for k in range(wides - 1):
            coarse_copy(o, h, turn_of(k)).start()

    def receive(t, h, kind):
        for d in range(1, wides):
            exchange(t, h, d).wait_recv()
        pieces = []
        for d in range(wides):
            pieces.extend(dup(land[lax.rem(t, 2), h, d]))
        rhs = mix(jnp.concatenate(pieces, axis=0))
        if kind == "coarse":
            coarse_send(t // INNER, h, rhs)
        res = res_d[h, :shared, :] + fold(mat(scatter[...], rhs))
        res_d[h, :shared, :] = res
        if kind == "plain":
            return advance(0, h, 0.3 * res)
        mult_d[h, :shared, :] += 0.3 * res

    def select(h, rhs):
        return fold(pre_sel[h] + mat(sel_hi[:, :shared], rhs) + mat(sel_lo[:, :shared], rhs))

    def solved_copy(o, h, d):
        return pltpu.make_async_remote_copy(
            src_ref=part.at[o, h, lax.rem(n + d, narrows)],
            dst_ref=solved_in.at[o, h, d],
            send_sem=n_send.at[o, h, d],
            recv_sem=n_recv.at[o, h, d],
            device_id={"narrow": lax.rem(n + d, narrows)},
            device_id_type=MESH,
        )

    def coarse_mid(o, h):
        for d in range(1, wides):
            coarse_copy(o, h, d).wait_recv()
        pieces = []
        for k in range(wides):
            pieces.extend(dup(coarse_all[o, h, k]))
        both = mat(inv_hl[...], mix(jnp.concatenate(pieces, axis=0)))
        size = narrows * modes
        p = fold(both[:size] + both[size:])
        first = low((modes // 2, loads))
        for k in range(narrows):
            part[o, h, k] = jnp.where(
                first,
                p[k * modes : k * modes + modes // 2],
                p[k * modes + modes // 2 : (k + 1) * modes],
            )
        for d in range(1, narrows):
            solved_copy(o, h, d).start()

    def coarse_end(o, h):
        total = part[o, h, n]
        for d in range(1, narrows):
            solved_copy(o, h, d).wait_recv()
            total = total + solved_in[o, h, d]
        s = mix(jnp.concatenate(dup(total), axis=0))
        s = jnp.concatenate([s, s], axis=0)

        lift = fold(mat(modes_t[...], s))
        for b in range(blocks):
            advance(b, h, lift[b * shared : (b + 1) * shared])
        return fold(mat(choose[...], mix(fold(top_of(h, 0, order)))))

    split_rows(0)
    for h in range(2):
        pre_top[h] = fold(top_of(h, 0, order))
    for b in range(1, blocks):
        split_rows(b)
    loads_of[1 + blocks].wait()
    for h, x in enumerate(dup(gap_f32[...])):
        gap_d[h] = x
    wall = jnp.where(contact_ref[...] == 1, 0.0, -jnp.inf)
    floor_d[...] = jnp.broadcast_to(wall, (loads, order)).T
    loads_of[2 + blocks].wait()
    m = modes_f32[...]
    m_hi = m.astype(BF16).astype(F32)
    modes_hl[:modes, :] = m.astype(BF16)
    modes_hl[modes:, :] = (m - m_hi).astype(BF16)
    modes_t[...] = jnp.concatenate([m_hi, m - m_hi], axis=0).T.astype(BF16)
    pieces = [wanted[:, :cap]]
    for d in range(1, wides):
        idx_copies[d - 1].wait_recv()
        pieces.append(idx_in[d, 0:1, :])
    index = jnp.concatenate(pieces, axis=1)
    rowid = lax.broadcasted_iota(jnp.int32, (shared, slots), 0).astype(F32)
    choose[...] = (
        jnp.where(rowid == jnp.broadcast_to(index, (shared, slots)), 1.0, 0.0).T.astype(BF16)
    )

    for h in range(2):
        send(0, h, fold(mat(choose[...], mix(pre_top[h]))))
    sel_hi[...] = mat(choose[...], op_hi[:shared, :]).astype(BF16)
    sel_lo[...] = mat(choose[...], op_lo[:shared, :]).astype(BF16)
    bottom("coarse", False)
    modes_s[...] = mat(modes_hl[:, :shared], scatter[...]).astype(BF16)
    loads_of[3 + blocks].wait()
    inv = inv_f32[...]
    inv_hi = inv.astype(BF16)
    size = narrows * modes
    inv_hl[:size, :] = inv_hi
    inv_hl[size:, :] = (inv - inv_hi.astype(F32)).astype(BF16)

    def emit(rows):
        first = low((rows.stop - rows.start, loads))
        mult_out[rows, :] = jnp.where(first, mult_d[0, rows, :], mult_d[1, rows, :])
        res_out[rows, :] = jnp.where(first, res_d[0, rows, :], res_d[1, rows, :])

    @pl.loop(0, OUTER)
    def _(o):
        t = o * INNER
        for h in range(2):
            receive(t, h, "coarse")
        for h in range(2):
            coarse_mid(o, h)
        for h in range(2):
            chosen = coarse_end(o, h)
            free(t, h)
            send(t + 1, h, chosen)
        bottom("plain", False)

        @pl.loop(1, INNER - 1)
        def _(i):
            for h in range(2):
                chosen = select(h, receive(t + i, h, "plain"))
                free(t + i, h)
                send(t + i + 1, h, chosen)
            bottom("plain", (o == OUTER - 1) & (i == INNER - 2))

        @pl.when(o == OUTER - 1)
        def _():
            emit(slice(shared, order))

        for h in range(2):
            mixed = receive(t + INNER - 1, h, "plain")

            @pl.when(o < OUTER - 1)
            def _():
                chosen = select(h, mixed)
                free(t + INNER - 1, h)
                send(t + INNER, h, chosen)

        @pl.when(o < OUTER - 1)
        def _():
            bottom("coarse", False)

    emit(slice(0, shared))
    for copy in idx_copies:
        copy.wait_send()
    for h in range(2):
        for d in range(1, wides):
            exchange(steps - 1, h, d).wait_send()
    for o in range(OUTER):
        for h in range(2):
            for d in range(1, wides):
                coarse_copy(o, h, d).wait_send()
            for d in range(1, narrows):
                solved_copy(o, h, d).wait_send()


def flush(mult, residual, mult_hbm, residual_hbm, sem):
    copies = [
        pltpu.make_async_copy(mult, mult_hbm, sem.at[0]),
        pltpu.make_async_copy(residual, residual_hbm, sem.at[1]),
    ]
    for copy in copies:
        copy.start()
    for copy in copies:
        copy.wait()


def local(
    wides,
    narrows,
    operators,
    coarse_inverse,
    modes,
    gap,
    start_mult,
    peer_list,
    partner_row,
    interface_size,
    contact_rows,
):
    order, loads = gap.shape[1:]
    shared = partner_row.shape[1]
    count = modes.shape[1]
    slots = 2 * shared
    cap = slots // wides
    far = pl.BlockSpec(memory_space=pltpu.HBM)
    near = pl.BlockSpec(memory_space=pltpu.VMEM)
    out = jax.ShapeDtypeStruct((order, loads), F32)
    held = pltpu.VMEM((order, loads), F32)
    dma = pltpu.SemaphoreType.DMA
    mult, residual = pl.pallas_call(
        functools.partial(kernel, wides, narrows),
        out_shape=(held, held),
        in_specs=[far] * 7 + [pl.BlockSpec(memory_space=pltpu.SMEM), far],
        out_specs=(near, near),
        scratch_shapes=[
            pltpu.VMEM((order, order), F32),
            pltpu.VMEM((order, order), BF16),
            pltpu.VMEM((order, order), BF16),
            pltpu.VMEM(coarse_inverse.shape, F32),
            pltpu.VMEM((2 * coarse_inverse.shape[0], coarse_inverse.shape[1]), BF16),
            pltpu.VMEM((count, order), F32),
            pltpu.VMEM((2 * count, order), BF16),
            pltpu.VMEM((order, 2 * count), BF16),
            pltpu.VMEM((order, loads), F32),
            pltpu.VMEM((order, loads), F32),
            pltpu.VMEM((2, order, loads), F32),
            pltpu.VMEM((order, loads), F32),
            pltpu.VMEM((2, order, loads), F32),
            pltpu.VMEM((2, order, loads), F32),
            pltpu.VMEM((order, 2 * loads), BF16),
            pltpu.VMEM((slots, shared), BF16),
            pltpu.VMEM((shared, slots), BF16),
            pltpu.VMEM((wides, 8, cap), F32),
            pltpu.VMEM((wides, 8, cap), F32),
            pltpu.VMEM((2, 2, wides, cap // 2, loads), F32),
            pltpu.VMEM((2, 2, wides, cap // 2, loads), F32),
            pltpu.VMEM((OUTER, 2, wides, count // 2, loads), F32),
            pltpu.VMEM((OUTER, 2, narrows, count // 2, loads), F32),
            pltpu.VMEM((OUTER, 2, narrows, count // 2, loads), F32),
            pltpu.VMEM((1, shared), jnp.int32),
            pltpu.VMEM((1, shared), jnp.int32),
            pltpu.VMEM((1, order), jnp.int32),
            pltpu.VMEM((2, shared, loads), F32),
            pltpu.VMEM((2, slots, loads), F32),
            pltpu.VMEM((2, 2 * count, loads), F32),
            pltpu.VMEM((slots, order), BF16),
            pltpu.VMEM((slots, order), BF16),
            pltpu.VMEM((2 * count, slots), BF16),
            dma((7 + order // shared,)),
            dma((wides,)),
            dma((wides,)),
            dma((2, 2, wides)),
            dma((2, 2, wides)),
            dma((OUTER, 2, wides)),
            dma((OUTER, 2, wides)),
            dma((OUTER, 2, narrows)),
            dma((OUTER, 2, narrows)),
        ],
        compiler_params=pltpu.CompilerParams(
            collective_id=0, has_side_effects=True, vmem_limit_bytes=67043328 - 2 * order * loads * 4
        ),
        name="feti",
    )(
        operators[0],
        coarse_inverse,
        modes[0],
        gap[0],
        start_mult[0],
        peer_list.reshape(1, shared),
        partner_row,
        interface_size,
        contact_rows,
    )
    mult, residual = pl.pallas_call(
        flush,
        out_shape=(out, out),
        in_specs=[near] * 2,
        out_specs=(far, far),
        scratch_shapes=[dma((2,))],
        compiler_params=pltpu.CompilerParams(vmem_limit_bytes=2**20),
        name="flush",
    )(mult, residual)
    return (mult[None], residual[None])


def solution(mesh):
    everyone = ("groups", "wide", "narrow")
    return jax.shard_map(
        functools.partial(local, mesh.shape["wide"], mesh.shape["narrow"]),
        mesh=mesh,
        in_specs=(
            P(everyone, None, None),
            P(("groups", "wide"), "narrow"),
            P(everyone, None, None),
            P(everyone, None, None),
            P(everyone, None, None),
            P(everyone, None, None),
            P(everyone, None),
            P(everyone),
            P(everyone, None),
        ),
        out_specs=(P(everyone, None, None), P(everyone, None, None)),
        check_vma=False,
    )
```

```python
import functools

import jax
import jax.numpy as jnp
from jax import lax
from jax.experimental import pallas as pl
from jax.experimental.pallas import tpu as pltpu
from jax.sharding import PartitionSpec as P

OUTER = 2
INNER = 3
F32 = jnp.float32
BF16 = jnp.bfloat16
MESH = pl.DeviceIdType.MESH


def kernel(
    wides,
    narrows,
    operator_hbm,
    inverse_hbm,
    modes_hbm,
    gap_hbm,
    start_hbm,
    peers_hbm,
    partner_hbm,
    size_ref,
    contact_hbm,
    mult_out,
    res_out,
    op_f32,
    op_hi,
    op_lo,
    inv_f32,
    inv_hl,
    modes_f32,
    modes_hl,
    modes_t,
    gap_f32,
    start_f32,
    gap_d,
    floor_d,
    mult_d,
    res_d,
    mix_d,
    choose,
    scatter,
    idx_out,
    idx_in,
    pack,
    land,
    coarse_all,
    part,
    solved_in,
    peers_ref,
    partner_ref,
    contact_ref,
    pre_top,
    pre_sel,
    pre_coarse,
    sel_hi,
    sel_lo,
    modes_s,
    load_sem,
    idx_send,
    idx_recv,
    x_send,
    x_recv,
    c_send,
    c_recv,
    n_send,
    n_recv,
):
    order, loads = gap_f32.shape
    shared = peers_ref.shape[1]
    modes = modes_f32.shape[0]
    half = loads // 2
    slots = scatter.shape[1]
    cap = slots // wides
    blocks = order // shared
    w = lax.axis_index("wide")
    n = lax.axis_index("narrow")

    barrier = pltpu.get_barrier_semaphore()
    for d in range(1, wides):
        pl.semaphore_signal(
            barrier, inc=1, device_id={"wide": lax.rem(w + d, wides)}, device_id_type=MESH
        )
    for d in range(1, narrows):
        pl.semaphore_signal(
            barrier, inc=1, device_id={"narrow": lax.rem(n + d, narrows)}, device_id_type=MESH
        )

    def load(src, dst, k):
        return pltpu.make_async_copy(src, dst, load_sem.at[k])

    small = [
        load(peers_hbm, peers_ref, 4 + blocks),
        load(partner_hbm, partner_ref, 5 + blocks),
        load(contact_hbm, contact_ref, 6 + blocks),
    ]
    for copy in small:
        copy.start()
    loads_of = [load(start_hbm, start_f32, 0)]
    for b in range(blocks):
        rows = pl.ds(b * shared, shared)
        loads_of.append(load(operator_hbm.at[rows], op_f32.at[rows], 1 + b))
    loads_of.append(load(gap_hbm, gap_f32, 1 + blocks))
    loads_of.append(load(modes_hbm, modes_f32, 2 + blocks))
    loads_of.append(load(inverse_hbm, inv_f32, 3 + blocks))
    for copy in loads_of:
        copy.start()

    for copy in small:
        copy.wait()
    peer_row = peers_ref[...].astype(F32)
    peer_col = jnp.broadcast_to(peer_row, (loads, shared)).T[:, :1]
    before = lax.broadcasted_iota(jnp.int32, (shared, shared), 1) < lax.broadcasted_iota(
        jnp.int32, (shared, shared), 0
    )
    same = jnp.broadcast_to(peer_row, (shared, shared)) == peer_col
    rank = jnp.sum(jnp.where(before & same, 1.0, 0.0), axis=1, keepdims=True)
    ahead = peer_col - w.astype(F32)
    ahead = jnp.where(ahead < 0.0, ahead + float(wides), ahead)
    target = jnp.broadcast_to(ahead * float(cap) + rank, (shared, slots))
    column = lax.broadcasted_iota(jnp.int32, (shared, slots), 1).astype(F32)
    partner_col = jnp.broadcast_to(partner_ref[...].astype(F32), (loads, shared)).T[:, :1]
    wanted = jnp.sum(
        jnp.where(target == column, jnp.broadcast_to(partner_col, (shared, slots)), 0.0),
        axis=0,
        keepdims=True,
    )
    for d in range(wides):
        idx_out[d] = jnp.broadcast_to(wanted[:, d * cap : (d + 1) * cap], idx_out.shape[1:])
    pl.semaphore_wait(barrier, wides - 1 + narrows - 1)
    idx_copies = []
    for d in sorted(range(1, wides), key=lambda d: -min(d, wides - d)):
        copy = pltpu.make_async_remote_copy(
            src_ref=idx_out.at[d],
            dst_ref=idx_in.at[d],
            send_sem=idx_send.at[d],
            recv_sem=idx_recv.at[d],
            device_id={"wide": lax.rem(w + d, wides)},
            device_id_type=MESH,
        )
        copy.start()
        idx_copies.append(copy)
    live = lax.broadcasted_iota(jnp.int32, (shared, slots), 0) < size_ref[0]
    scatter[...] = jnp.where((target == column) & live, 1.0, 0.0).astype(BF16)

    def low(shape):
        return lax.broadcasted_iota(jnp.int32, shape, 1) < half

    def mix(x):
        return jnp.where(low(x.shape), x, x - x.astype(BF16).astype(F32)).astype(BF16)

    def turn(x):
        return pltpu.roll(x, half, 1)

    def fold(x):
        return x + turn(x)

    def dup(x):
        y = turn(x)
        m = low(x.shape)
        return jnp.where(m, x, y), jnp.where(m, y, x)

    def mat(a, b):
        return jnp.dot(a, b, preferred_element_type=F32)

    def side(h):
        return slice(h * loads, (h + 1) * loads)

    loads_of[0].wait()
    for h, x in enumerate(dup(start_f32[...])):
        mult_d[h] = x
        mix_d[:, side(h)] = mix(x)

    steps = OUTER * INNER

    def split_rows(b):
        loads_of[1 + b].wait()
        x = op_f32[pl.ds(b * shared, shared), :]
        hi = x.astype(BF16)
        op_hi[pl.ds(b * shared, shared), :] = hi
        op_lo[pl.ds(b * shared, shared), :] = (x - hi.astype(F32)).astype(BF16)

    def active(b):
        return (
            b * shared + lax.broadcasted_iota(jnp.int32, (shared, loads), 0)
        ) < size_ref[0]

    def top_of(h, first, last):
        rhs = mix_d[first:last, side(h)]
        return mat(op_hi[:shared, first:last], rhs) + mat(op_lo[:shared, first:last], rhs)

    def exchange(t, h, k):
        slot = lax.rem(t, 2)
        return pltpu.make_async_remote_copy(
            src_ref=pack.at[slot, h, k],
            dst_ref=land.at[slot, h, turn_of(wides - 2 - k)],
            send_sem=x_send.at[slot, h, k],
            recv_sem=x_recv.at[slot, h, turn_of(wides - 2 - k)],
            device_id={"wide": peer(wides - 2 - k)},
            device_id_type=MESH,
        )

    def peer(k):
        up = wides - 2 - k + jnp.where(wides - 2 - k >= w, 1, 0)
        down = k + 1 - jnp.where(k + 1 <= w, 1, 0)
        return jnp.where(w < wides // 2, down, up)

    def turn_of(k):
        return lax.rem(w + wides - peer(k), wides)


    def send(t, h, chosen):
        first = low((cap // 2, loads))
        for k in range(wides):
            value = jnp.where(
                first,
                chosen[k * cap : k * cap + cap // 2],
                chosen[k * cap + cap // 2 : (k + 1) * cap],
            )
            if k == wides - 1:
                land[lax.rem(t, 2), h, 0] = value
            else:
                pack[lax.rem(t, 2), h, k] = value
                exchange(t, h, k).start()

    def advance(b, h, update):
        rows = pl.ds(b * shared, shared)
        if not isinstance(b, int):
            rows = pl.ds(pl.multiple_of(b * shared, shared), shared)
        trial = jnp.maximum(mult_d[h, rows, :] + update, floor_d[rows, :])
        new = jnp.where(active(b), trial, 0.0)
        mixed = mix(new)
        mult_d[h, rows, :] = new
        mix_d[rows, side(h)] = mixed
        return mixed

    def free(t, h):
        for k in range(wides - 1):
            exchange(t, h, k).wait_send()

    def bottom(kind, last):
        @pl.loop(0, blocks)
        def _(b):
            rows = pl.ds(pl.multiple_of(b * shared, shared), shared)
            rhs = mix_d[...]
            image = mat(op_hi[rows, :], rhs) + mat(op_lo[rows, :], rhs)
            for h in range(2):
                res_d[h, rows, :] = jnp.where(
                    active(b), gap_d[h, rows, :] - fold(image[:, side(h)]), 0.0
                )

        if kind == "plain":

            @pl.loop(1, blocks)
            def _(b):
                rows = pl.ds(pl.multiple_of(b * shared, shared), shared)
                for h in range(2):
                    advance(b, h, 0.3 * res_d[h, rows, :])

            @pl.when(jnp.logical_not(last))
            def _():
                rhs = mix_d[shared:, :]
                pre = mat(sel_hi[:, shared:], rhs) + mat(sel_lo[:, shared:], rhs)
                for h in range(2):
                    pre_sel[h] = pre[:, side(h)]
        else:
            rhs = jnp.concatenate([mix(res_d[h]) for h in range(2)], axis=1)
            pre = mat(modes_hl[...], rhs)
            for h in range(2):
                mult_d[h, shared:, :] += 0.3 * res_d[h, shared:, :]
            for h in range(2):
                pre_coarse[h] = pre[:, side(h)]

    def coarse_copy(o, h, d):
        return pltpu.make_async_remote_copy(
            src_ref=coarse_all.at[o, h, w],
            dst_ref=coarse_all.at[o, h, w],
            send_sem=c_send.at[o, h, d],
            recv_sem=c_recv.at[o, h, d],
            device_id={"wide": lax.rem(w + wides - d, wides)},
            device_id_type=MESH,
        )

    def coarse_send(o, h, rhs):
        both = pre_coarse[h] + mat(modes_s[...], rhs)
        c = fold(both[:modes] + both[modes:])
        coarse_all[o, h, w] = jnp.where(
            low((modes // 2, loads)), c[: modes // 2], c[modes // 2 :]
        )
        for k in range(wides - 1):
            coarse_copy(o, h, turn_of(k)).start()

    def receive(t, h, kind):
        for k in range(wides - 1):
            exchange(t, h, k).wait_recv()
        pieces = []
        for d in range(wides):
            pieces.extend(dup(land[lax.rem(t, 2), h, d]))
        rhs = mix(jnp.concatenate(pieces, axis=0))
        if kind == "coarse":
            coarse_send(t // INNER, h, rhs)
        res = res_d[h, :shared, :] + fold(mat(scatter[...], rhs))
        res_d[h, :shared, :] = res
        if kind == "plain":
            return advance(0, h, 0.3 * res)
        mult_d[h, :shared, :] += 0.3 * res

    def select(h, rhs):
        return fold(pre_sel[h] + mat(sel_hi[:, :shared], rhs) + mat(sel_lo[:, :shared], rhs))

    def solved_copy(o, h, d):
        return pltpu.make_async_remote_copy(
            src_ref=part.at[o, h, lax.rem(n + d, narrows)],
            dst_ref=solved_in.at[o, h, d],
            send_sem=n_send.at[o, h, d],
            recv_sem=n_recv.at[o, h, d],
            device_id={"narrow": lax.rem(n + d, narrows)},
            device_id_type=MESH,
        )

    def coarse_mid(o, h):
        for d in range(1, wides):
            coarse_copy(o, h, d).wait_recv()
        pieces = []
        for k in range(wides):
            pieces.extend(dup(coarse_all[o, h, k]))
        both = mat(inv_hl[...], mix(jnp.concatenate(pieces, axis=0)))
        size = narrows * modes
        p = fold(both[:size] + both[size:])
        first = low((modes // 2, loads))
        for k in range(narrows):
            part[o, h, k] = jnp.where(
                first,
                p[k * modes : k * modes + modes // 2],
                p[k * modes + modes // 2 : (k + 1) * modes],
            )
        for d in sorted(range(1, narrows), key=lambda d: -min(d, narrows - d)):
            solved_copy(o, h, d).start()

    def coarse_end(o, h):
        total = part[o, h, n]
        for d in range(1, narrows):
            solved_copy(o, h, d).wait_recv()
            total = total + solved_in[o, h, d]
        s = mix(jnp.concatenate(dup(total), axis=0))
        s = jnp.concatenate([s, s], axis=0)

        lift = fold(mat(modes_t[...], s))
        for b in range(blocks):
            advance(b, h, lift[b * shared : (b + 1) * shared])
        return fold(mat(choose[...], mix(fold(top_of(h, 0, order)))))

    split_rows(0)
    for h in range(2):
        pre_top[h] = fold(top_of(h, 0, order))
    for b in range(1, blocks):
        split_rows(b)
    loads_of[1 + blocks].wait()
    for h, x in enumerate(dup(gap_f32[...])):
        gap_d[h] = x
    wall = jnp.where(contact_ref[...] == 1, 0.0, -jnp.inf)
    floor_d[...] = jnp.broadcast_to(wall, (loads, order)).T
    loads_of[2 + blocks].wait()
    m = modes_f32[...]
    m_hi = m.astype(BF16).astype(F32)
    modes_hl[:modes, :] = m.astype(BF16)
    modes_hl[modes:, :] = (m - m_hi).astype(BF16)
    modes_t[...] = jnp.concatenate([m_hi, m - m_hi], axis=0).T.astype(BF16)
    for copy in idx_copies:
        copy.wait_recv()
    pieces = []
    for k in range(wides - 1):
        pieces.append(idx_in[turn_of(wides - 2 - k), 0:1, :])
    pieces.append(wanted[:, :cap])
    index = jnp.concatenate(pieces, axis=1)
    rowid = lax.broadcasted_iota(jnp.int32, (shared, slots), 0).astype(F32)
    choose[...] = (
        jnp.where(rowid == jnp.broadcast_to(index, (shared, slots)), 1.0, 0.0).T.astype(BF16)
    )

    for h in range(2):
        send(0, h, fold(mat(choose[...], mix(pre_top[h]))))
    sel_hi[...] = mat(choose[...], op_hi[:shared, :]).astype(BF16)
    sel_lo[...] = mat(choose[...], op_lo[:shared, :]).astype(BF16)
    bottom("coarse", False)
    modes_s[...] = mat(modes_hl[:, :shared], scatter[...]).astype(BF16)
    loads_of[3 + blocks].wait()
    inv = inv_f32[...]
    inv_hi = inv.astype(BF16)
    size = narrows * modes
    inv_hl[:size, :] = inv_hi
    inv_hl[size:, :] = (inv - inv_hi.astype(F32)).astype(BF16)

    def emit(rows):
        first = low((rows.stop - rows.start, loads))
        mult_out[rows, :] = jnp.where(first, mult_d[0, rows, :], mult_d[1, rows, :])
        res_out[rows, :] = jnp.where(first, res_d[0, rows, :], res_d[1, rows, :])

    @pl.loop(0, OUTER)
    def _(o):
        t = o * INNER
        for h in range(2):
            receive(t, h, "coarse")
        for h in range(2):
            coarse_mid(o, h)
        for h in range(2):
            chosen = coarse_end(o, h)
            free(t, h)
            send(t + 1, h, chosen)
        bottom("plain", False)

        @pl.loop(1, INNER - 1)
        def _(i):
            for h in range(2):
                chosen = select(h, receive(t + i, h, "plain"))
                free(t + i, h)
                send(t + i + 1, h, chosen)
            bottom("plain", (o == OUTER - 1) & (i == INNER - 2))

        @pl.when(o == OUTER - 1)
        def _():
            emit(slice(shared, order))

        for h in range(2):
            mixed = receive(t + INNER - 1, h, "plain")

            @pl.when(o < OUTER - 1)
            def _():
                chosen = select(h, mixed)
                free(t + INNER - 1, h)
                send(t + INNER, h, chosen)

        @pl.when(o < OUTER - 1)
        def _():
            bottom("coarse", False)

    emit(slice(0, shared))
    for copy in idx_copies:
        copy.wait_send()
    for h in range(2):
        for k in range(wides - 1):
            exchange(steps - 1, h, k).wait_send()
    for o in range(OUTER):
        for h in range(2):
            for d in range(1, wides):
                coarse_copy(o, h, d).wait_send()
            for d in range(1, narrows):
                solved_copy(o, h, d).wait_send()


def flush(mult, residual, mult_hbm, residual_hbm, sem):
    copies = [
        pltpu.make_async_copy(mult, mult_hbm, sem.at[0]),
        pltpu.make_async_copy(residual, residual_hbm, sem.at[1]),
    ]
    for copy in copies:
        copy.start()
    for copy in copies:
        copy.wait()


def local(
    wides,
    narrows,
    operators,
    coarse_inverse,
    modes,
    gap,
    start_mult,
    peer_list,
    partner_row,
    interface_size,
    contact_rows,
):
    order, loads = gap.shape[1:]
    shared = partner_row.shape[1]
    count = modes.shape[1]
    slots = 2 * shared
    cap = slots // wides
    far = pl.BlockSpec(memory_space=pltpu.HBM)
    near = pl.BlockSpec(memory_space=pltpu.VMEM)
    out = jax.ShapeDtypeStruct((order, loads), F32)
    held = pltpu.VMEM((order, loads), F32)
    dma = pltpu.SemaphoreType.DMA
    mult, residual = pl.pallas_call(
        functools.partial(kernel, wides, narrows),
        out_shape=(held, held),
        in_specs=[far] * 7 + [pl.BlockSpec(memory_space=pltpu.SMEM), far],
        out_specs=(near, near),
        scratch_shapes=[
            pltpu.VMEM((order, order), F32),
            pltpu.VMEM((order, order), BF16),
            pltpu.VMEM((order, order), BF16),
            pltpu.VMEM(coarse_inverse.shape, F32),
            pltpu.VMEM((2 * coarse_inverse.shape[0], coarse_inverse.shape[1]), BF16),
            pltpu.VMEM((count, order), F32),
            pltpu.VMEM((2 * count, order), BF16),
            pltpu.VMEM((order, 2 * count), BF16),
            pltpu.VMEM((order, loads), F32),
            pltpu.VMEM((order, loads), F32),
            pltpu.VMEM((2, order, loads), F32),
            pltpu.VMEM((order, loads), F32),
            pltpu.VMEM((2, order, loads), F32),
            pltpu.VMEM((2, order, loads), F32),
            pltpu.VMEM((order, 2 * loads), BF16),
            pltpu.VMEM((slots, shared), BF16),
            pltpu.VMEM((shared, slots), BF16),
            pltpu.VMEM((wides, 8, cap), F32),
            pltpu.VMEM((wides, 8, cap), F32),
            pltpu.VMEM((2, 2, wides, cap // 2, loads), F32),
            pltpu.VMEM((2, 2, wides, cap // 2, loads), F32),
            pltpu.VMEM((OUTER, 2, wides, count // 2, loads), F32),
            pltpu.VMEM((OUTER, 2, narrows, count // 2, loads), F32),
            pltpu.VMEM((OUTER, 2, narrows, count // 2, loads), F32),
            pltpu.VMEM((1, shared), jnp.int32),
            pltpu.VMEM((1, shared), jnp.int32),
            pltpu.VMEM((1, order), jnp.int32),
            pltpu.VMEM((2, shared, loads), F32),
            pltpu.VMEM((2, slots, loads), F32),
            pltpu.VMEM((2, 2 * count, loads), F32),
            pltpu.VMEM((slots, order), BF16),
            pltpu.VMEM((slots, order), BF16),
            pltpu.VMEM((2 * count, slots), BF16),
            dma((7 + order // shared,)),
            dma((wides,)),
            dma((wides,)),
            dma((2, 2, wides)),
            dma((2, 2, wides)),
            dma((OUTER, 2, wides)),
            dma((OUTER, 2, wides)),
            dma((OUTER, 2, narrows)),
            dma((OUTER, 2, narrows)),
        ],
        compiler_params=pltpu.CompilerParams(
            collective_id=0, has_side_effects=True, vmem_limit_bytes=67043328 - 2 * order * loads * 4
        ),
        name="feti",
    )(
        operators[0],
        coarse_inverse,
        modes[0],
        gap[0],
        start_mult[0],
        peer_list.reshape(1, shared),
        partner_row,
        interface_size,
        contact_rows,
    )
    mult, residual = pl.pallas_call(
        flush,
        out_shape=(out, out),
        in_specs=[near] * 2,
        out_specs=(far, far),
        scratch_shapes=[dma((2,))],
        compiler_params=pltpu.CompilerParams(vmem_limit_bytes=2**20),
        name="flush",
    )(mult, residual)
    return (mult[None], residual[None])


def solution(mesh):
    everyone = ("groups", "wide", "narrow")
    return jax.shard_map(
        functools.partial(local, mesh.shape["wide"], mesh.shape["narrow"]),
        mesh=mesh,
        in_specs=(
            P(everyone, None, None),
            P(("groups", "wide"), "narrow"),
            P(everyone, None, None),
            P(everyone, None, None),
            P(everyone, None, None),
            P(everyone, None, None),
            P(everyone, None),
            P(everyone),
            P(everyone, None),
        ),
        out_specs=(P(everyone, None, None), P(everyone, None, None)),
        check_vma=False,
    )
```

```python
import functools

import jax
import jax.numpy as jnp
from jax import lax
from jax.experimental import pallas as pl
from jax.experimental.pallas import tpu as pltpu
from jax.sharding import PartitionSpec as P

OUTER = 2
INNER = 3
F32 = jnp.float32
BF16 = jnp.bfloat16
MESH = pl.DeviceIdType.MESH


def kernel(
    wides,
    narrows,
    operator_hbm,
    inverse_hbm,
    modes_hbm,
    gap_hbm,
    start_hbm,
    peers_hbm,
    partner_hbm,
    size_ref,
    contact_hbm,
    mult_out,
    res_out,
    op_f32,
    op_hi,
    op_lo,
    inv_f32,
    inv_hl,
    modes_f32,
    modes_hl,
    modes_t,
    gap_f32,
    start_f32,
    gap_d,
    floor_d,
    mult_d,
    res_d,
    mix_d,
    choose,
    scatter,
    idx_out,
    idx_in,
    pack,
    land,
    coarse_all,
    part,
    solved_in,
    peers_ref,
    partner_ref,
    contact_ref,
    pre_top,
    pre_sel,
    pre_coarse,
    sel_hi,
    sel_lo,
    modes_s,
    load_sem,
    idx_send,
    idx_recv,
    x_send,
    x_recv,
    c_send,
    c_recv,
    n_send,
    n_recv,
):
    order, loads = gap_f32.shape
    shared = peers_ref.shape[1]
    modes = modes_f32.shape[0]
    half = loads // 2
    slots = scatter.shape[1]
    cap = slots // wides
    blocks = order // shared
    w = lax.axis_index("wide")
    n = lax.axis_index("narrow")

    barrier = pltpu.get_barrier_semaphore()
    for d in range(1, wides):
        pl.semaphore_signal(
            barrier, inc=1, device_id={"wide": lax.rem(w + d, wides)}, device_id_type=MESH
        )
    for d in range(1, narrows):
        pl.semaphore_signal(
            barrier, inc=1, device_id={"narrow": lax.rem(n + d, narrows)}, device_id_type=MESH
        )

    def load(src, dst, k):
        return pltpu.make_async_copy(src, dst, load_sem.at[k])

    small = [
        load(peers_hbm, peers_ref, 4 + blocks),
        load(partner_hbm, partner_ref, 5 + blocks),
        load(contact_hbm, contact_ref, 6 + blocks),
    ]
    for copy in small:
        copy.start()
    loads_of = [load(start_hbm, start_f32, 0)]
    for b in range(blocks):
        rows = pl.ds(b * shared, shared)
        loads_of.append(load(operator_hbm.at[rows], op_f32.at[rows], 1 + b))
    loads_of.append(load(gap_hbm, gap_f32, 1 + blocks))
    loads_of.append(load(modes_hbm, modes_f32, 2 + blocks))
    loads_of.append(load(inverse_hbm, inv_f32, 3 + blocks))
    for copy in loads_of:
        copy.start()

    for copy in small:
        copy.wait()
    peer_row = peers_ref[...].astype(F32)
    peer_col = jnp.broadcast_to(peer_row, (loads, shared)).T[:, :1]
    before = lax.broadcasted_iota(jnp.int32, (shared, shared), 1) < lax.broadcasted_iota(
        jnp.int32, (shared, shared), 0
    )
    same = jnp.broadcast_to(peer_row, (shared, shared)) == peer_col
    rank = jnp.sum(jnp.where(before & same, 1.0, 0.0), axis=1, keepdims=True)
    ahead = peer_col - w.astype(F32)
    ahead = jnp.where(ahead < 0.0, ahead + float(wides), ahead)
    target = jnp.broadcast_to(ahead * float(cap) + rank, (shared, slots))
    column = lax.broadcasted_iota(jnp.int32, (shared, slots), 1).astype(F32)
    partner_col = jnp.broadcast_to(partner_ref[...].astype(F32), (loads, shared)).T[:, :1]
    wanted = jnp.sum(
        jnp.where(target == column, jnp.broadcast_to(partner_col, (shared, slots)), 0.0),
        axis=0,
        keepdims=True,
    )
    for d in range(wides):
        idx_out[d] = jnp.broadcast_to(wanted[:, d * cap : (d + 1) * cap], idx_out.shape[1:])
    pl.semaphore_wait(barrier, wides - 1 + narrows - 1)
    idx_copies = []
    for d in sorted(range(1, wides), key=lambda d: -min(d, wides - d)):
        copy = pltpu.make_async_remote_copy(
            src_ref=idx_out.at[d],
            dst_ref=idx_in.at[d],
            send_sem=idx_send.at[d],
            recv_sem=idx_recv.at[d],
            device_id={"wide": lax.rem(w + d, wides)},
            device_id_type=MESH,
        )
        copy.start()
        idx_copies.append(copy)
    live = lax.broadcasted_iota(jnp.int32, (shared, slots), 0) < size_ref[0]
    scatter[...] = jnp.where((target == column) & live, 1.0, 0.0).astype(BF16)

    def low(shape):
        return lax.broadcasted_iota(jnp.int32, shape, 1) < half

    def mix(x):
        return jnp.where(low(x.shape), x, x - x.astype(BF16).astype(F32)).astype(BF16)

    def turn(x):
        return pltpu.roll(x, half, 1)

    def fold(x):
        return x + turn(x)

    def dup(x):
        y = turn(x)
        m = low(x.shape)
        return jnp.where(m, x, y), jnp.where(m, y, x)

    def mat(a, b):
        return jnp.dot(a, b, preferred_element_type=F32)

    def side(h):
        return slice(h * loads, (h + 1) * loads)

    loads_of[0].wait()
    for h, x in enumerate(dup(start_f32[...])):
        mult_d[h] = x
        mix_d[:, side(h)] = mix(x)

    steps = OUTER * INNER

    def split_rows(b):
        loads_of[1 + b].wait()
        x = op_f32[pl.ds(b * shared, shared), :]
        hi = x.astype(BF16)
        op_hi[pl.ds(b * shared, shared), :] = hi
        op_lo[pl.ds(b * shared, shared), :] = (x - hi.astype(F32)).astype(BF16)

    def active(b):
        return (
            b * shared + lax.broadcasted_iota(jnp.int32, (shared, loads), 0)
        ) < size_ref[0]

    def top_of(h, first, last):
        rhs = mix_d[first:last, side(h)]
        return mat(op_hi[:shared, first:last], rhs) + mat(op_lo[:shared, first:last], rhs)

    def exchange(t, h, k):
        slot = lax.rem(t, 2)
        return pltpu.make_async_remote_copy(
            src_ref=pack.at[slot, h, k],
            dst_ref=land.at[slot, h, turn_of(wides - 2 - k)],
            send_sem=x_send.at[slot, h, k],
            recv_sem=x_recv.at[slot, h, turn_of(wides - 2 - k)],
            device_id={"wide": peer(wides - 2 - k)},
            device_id_type=MESH,
        )

    def peer(k):
        up = wides - 2 - k + jnp.where(wides - 2 - k >= w, 1, 0)
        down = k + 1 - jnp.where(k + 1 <= w, 1, 0)
        return jnp.where(w < wides // 2, down, up)

    def turn_of(k):
        return lax.rem(w + wides - peer(k), wides)


    def send(t, h, chosen):
        first = low((cap // 2, loads))
        for k in range(wides):
            value = jnp.where(
                first,
                chosen[k * cap : k * cap + cap // 2],
                chosen[k * cap + cap // 2 : (k + 1) * cap],
            )
            if k == wides - 1:
                land[lax.rem(t, 2), h, 0] = value
            else:
                pack[lax.rem(t, 2), h, k] = value
                exchange(t, h, k).start()

    def advance(b, h, update):
        rows = pl.ds(b * shared, shared)
        if not isinstance(b, int):
            rows = pl.ds(pl.multiple_of(b * shared, shared), shared)
        trial = jnp.maximum(mult_d[h, rows, :] + update, floor_d[rows, :])
        new = jnp.where(active(b), trial, 0.0)
        mixed = mix(new)
        mult_d[h, rows, :] = new
        mix_d[rows, side(h)] = mixed
        return mixed

    def free(t, h):
        for k in range(wides - 1):
            exchange(t, h, k).wait_send()

    def bottom(kind, last):
        @pl.loop(0, blocks)
        def _(b):
            rows = pl.ds(pl.multiple_of(b * shared, shared), shared)
            rhs = mix_d[...]
            image = mat(op_hi[rows, :], rhs) + mat(op_lo[rows, :], rhs)
            for h in range(2):
                res_d[h, rows, :] = jnp.where(
                    active(b), gap_d[h, rows, :] - fold(image[:, side(h)]), 0.0
                )

        if kind == "plain":

            @pl.loop(1, blocks)
            def _(b):
                rows = pl.ds(pl.multiple_of(b * shared, shared), shared)
                for h in range(2):
                    advance(b, h, 0.3 * res_d[h, rows, :])

            @pl.when(jnp.logical_not(last))
            def _():
                rhs = mix_d[shared:, :]
                pre = mat(sel_hi[:, shared:], rhs) + mat(sel_lo[:, shared:], rhs)
                for h in range(2):
                    pre_sel[h] = pre[:, side(h)]
        else:
            rhs = jnp.concatenate([mix(res_d[h]) for h in range(2)], axis=1)
            pre = mat(modes_hl[...], rhs)
            for h in range(2):
                mult_d[h, shared:, :] += 0.3 * res_d[h, shared:, :]
            for h in range(2):
                pre_coarse[h] = pre[:, side(h)]

    def coarse_copy(o, h, d):
        return pltpu.make_async_remote_copy(
            src_ref=coarse_all.at[o, h, w],
            dst_ref=coarse_all.at[o, h, w],
            send_sem=c_send.at[o, h, d],
            recv_sem=c_recv.at[o, h, d],
            device_id={"wide": lax.rem(w + wides - d, wides)},
            device_id_type=MESH,
        )

    def coarse_send(o, h, rhs):
        both = pre_coarse[h] + mat(modes_s[...], rhs)
        c = fold(both[:modes] + both[modes:])
        coarse_all[o, h, w] = jnp.where(
            low((modes // 2, loads)), c[: modes // 2], c[modes // 2 :]
        )
        for k in range(wides - 1):
            coarse_copy(o, h, turn_of(k)).start()

    def receive(t, h, kind):
        for k in range(wides - 1):
            exchange(t, h, k).wait_recv()
        pieces = []
        for d in range(wides):
            pieces.extend(dup(land[lax.rem(t, 2), h, d]))
        rhs = mix(jnp.concatenate(pieces, axis=0))
        if kind == "coarse":
            coarse_send(t // INNER, h, rhs)
        res = res_d[h, :shared, :] + fold(mat(scatter[...], rhs))
        res_d[h, :shared, :] = res
        if kind == "plain":
            return advance(0, h, 0.3 * res)
        mult_d[h, :shared, :] += 0.3 * res

    def select(h, rhs):
        return fold(pre_sel[h] + mat(sel_hi[:, :shared], rhs) + mat(sel_lo[:, :shared], rhs))

    def solved_copy(o, h, d):
        return pltpu.make_async_remote_copy(
            src_ref=part.at[o, h, lax.rem(n + d, narrows)],
            dst_ref=solved_in.at[o, h, d],
            send_sem=n_send.at[o, h, d],
            recv_sem=n_recv.at[o, h, d],
            device_id={"narrow": lax.rem(n + d, narrows)},
            device_id_type=MESH,
        )

    def coarse_mid(o, h):
        for d in range(1, wides):
            coarse_copy(o, h, d).wait_recv()
        pieces = []
        for k in range(wides):
            pieces.extend(dup(coarse_all[o, h, k]))
        both = mat(inv_hl[...], mix(jnp.concatenate(pieces, axis=0)))
        size = narrows * modes
        p = fold(both[:size] + both[size:])
        first = low((modes // 2, loads))
        for k in range(narrows):
            part[o, h, k] = jnp.where(
                first,
                p[k * modes : k * modes + modes // 2],
                p[k * modes + modes // 2 : (k + 1) * modes],
            )
        for d in sorted(range(1, narrows), key=lambda d: -min(d, narrows - d)):
            solved_copy(o, h, d).start()

    def coarse_end(o, h):
        total = part[o, h, n]
        for d in range(1, narrows):
            solved_copy(o, h, d).wait_recv()
            total = total + solved_in[o, h, d]
        s = mix(jnp.concatenate(dup(total), axis=0))
        s = jnp.concatenate([s, s], axis=0)

        lift = fold(mat(modes_t[...], s))
        for b in range(blocks):
            advance(b, h, lift[b * shared : (b + 1) * shared])
        return fold(mat(choose[...], mix(fold(top_of(h, 0, order)))))

    split_rows(0)
    for h in range(2):
        pre_top[h] = fold(top_of(h, 0, order))
    for b in range(1, blocks):
        split_rows(b)
    loads_of[1 + blocks].wait()
    for h, x in enumerate(dup(gap_f32[...])):
        gap_d[h] = x
    wall = jnp.where(contact_ref[...] == 1, 0.0, -jnp.inf)
    floor_d[...] = jnp.broadcast_to(wall, (loads, order)).T
    loads_of[2 + blocks].wait()
    m = modes_f32[...]
    m_hi = m.astype(BF16).astype(F32)
    modes_hl[:modes, :] = m.astype(BF16)
    modes_hl[modes:, :] = (m - m_hi).astype(BF16)
    modes_t[...] = jnp.concatenate([m_hi, m - m_hi], axis=0).T.astype(BF16)
    for copy in idx_copies:
        copy.wait_recv()
    pieces = []
    for k in range(wides - 1):
        pieces.append(idx_in[turn_of(wides - 2 - k), 0:1, :])
    pieces.append(wanted[:, :cap])
    index = jnp.concatenate(pieces, axis=1)
    rowid = lax.broadcasted_iota(jnp.int32, (shared, slots), 0).astype(F32)
    choose[...] = (
        jnp.where(rowid == jnp.broadcast_to(index, (shared, slots)), 1.0, 0.0).T.astype(BF16)
    )

    for h in range(2):
        send(0, h, fold(mat(choose[...], mix(pre_top[h]))))
    sel_hi[...] = mat(choose[...], op_hi[:shared, :]).astype(BF16)
    sel_lo[...] = mat(choose[...], op_lo[:shared, :]).astype(BF16)
    bottom("coarse", False)
    modes_s[...] = mat(modes_hl[:, :shared], scatter[...]).astype(BF16)
    loads_of[3 + blocks].wait()
    inv = inv_f32[...]
    inv_hi = inv.astype(BF16)
    size = narrows * modes
    inv_hl[:size, :] = inv_hi
    inv_hl[size:, :] = (inv - inv_hi.astype(F32)).astype(BF16)

    def emit(rows):
        first = low((rows.stop - rows.start, loads))
        mult_out[rows, :] = jnp.where(first, mult_d[0, rows, :], mult_d[1, rows, :])
        res_out[rows, :] = jnp.where(first, res_d[0, rows, :], res_d[1, rows, :])

    @pl.loop(0, OUTER)
    def _(o):
        t = o * INNER
        for h in range(2):
            receive(t, h, "coarse")
        for h in range(2):
            coarse_mid(o, h)
        for h in range(2):
            chosen = coarse_end(o, h)
            free(t, h)
            send(t + 1, h, chosen)
        bottom("plain", False)

        @pl.loop(1, INNER - 1)
        def _(i):
            for h in range(2):
                chosen = select(h, receive(t + i, h, "plain"))
                free(t + i, h)
                send(t + i + 1, h, chosen)
            bottom("plain", (o == OUTER - 1) & (i == INNER - 2))

        @pl.when(o == OUTER - 1)
        def _():
            emit(slice(shared, order))

        for h in range(2):
            mixed = receive(t + INNER - 1, h, "plain")

            @pl.when(o < OUTER - 1)
            def _():
                chosen = select(h, mixed)
                free(t + INNER - 1, h)
                send(t + INNER, h, chosen)

        @pl.when(o < OUTER - 1)
        def _():
            bottom("coarse", False)

    emit(slice(0, shared))
    for copy in idx_copies:
        copy.wait_send()
    for h in range(2):
        for k in range(wides - 1):
            exchange(steps - 1, h, k).wait_send()
    for o in range(OUTER):
        for h in range(2):
            for d in range(1, wides):
                coarse_copy(o, h, d).wait_send()
            for d in range(1, narrows):
                solved_copy(o, h, d).wait_send()


def flush(mult, residual, mult_hbm, residual_hbm, sem):
    rows = mult.shape[0] // 4
    copies = []
    for k in range(4):
        at = pl.ds(k * rows, rows)
        copies.append(pltpu.make_async_copy(mult.at[at], mult_hbm.at[at], sem.at[0, k]))
        copies.append(pltpu.make_async_copy(residual.at[at], residual_hbm.at[at], sem.at[1, k]))
    for copy in copies:
        copy.start()
    for copy in copies:
        copy.wait()


def local(
    wides,
    narrows,
    operators,
    coarse_inverse,
    modes,
    gap,
    start_mult,
    peer_list,
    partner_row,
    interface_size,
    contact_rows,
):
    order, loads = gap.shape[1:]
    shared = partner_row.shape[1]
    count = modes.shape[1]
    slots = 2 * shared
    cap = slots // wides
    far = pl.BlockSpec(memory_space=pltpu.HBM)
    near = pl.BlockSpec(memory_space=pltpu.VMEM)
    out = jax.ShapeDtypeStruct((order, loads), F32)
    held = pltpu.VMEM((order, loads), F32)
    dma = pltpu.SemaphoreType.DMA
    mult, residual = pl.pallas_call(
        functools.partial(kernel, wides, narrows),
        out_shape=(held, held),
        in_specs=[far] * 7 + [pl.BlockSpec(memory_space=pltpu.SMEM), far],
        out_specs=(near, near),
        scratch_shapes=[
            pltpu.VMEM((order, order), F32),
            pltpu.VMEM((order, order), BF16),
            pltpu.VMEM((order, order), BF16),
            pltpu.VMEM(coarse_inverse.shape, F32),
            pltpu.VMEM((2 * coarse_inverse.shape[0], coarse_inverse.shape[1]), BF16),
            pltpu.VMEM((count, order), F32),
            pltpu.VMEM((2 * count, order), BF16),
            pltpu.VMEM((order, 2 * count), BF16),
            pltpu.VMEM((order, loads), F32),
            pltpu.VMEM((order, loads), F32),
            pltpu.VMEM((2, order, loads), F32),
            pltpu.VMEM((order, loads), F32),
            pltpu.VMEM((2, order, loads), F32),
            pltpu.VMEM((2, order, loads), F32),
            pltpu.VMEM((order, 2 * loads), BF16),
            pltpu.VMEM((slots, shared), BF16),
            pltpu.VMEM((shared, slots), BF16),
            pltpu.VMEM((wides, 8, cap), F32),
            pltpu.VMEM((wides, 8, cap), F32),
            pltpu.VMEM((2, 2, wides, cap // 2, loads), F32),
            pltpu.VMEM((2, 2, wides, cap // 2, loads), F32),
            pltpu.VMEM((OUTER, 2, wides, count // 2, loads), F32),
            pltpu.VMEM((OUTER, 2, narrows, count // 2, loads), F32),
            pltpu.VMEM((OUTER, 2, narrows, count // 2, loads), F32),
            pltpu.VMEM((1, shared), jnp.int32),
            pltpu.VMEM((1, shared), jnp.int32),
            pltpu.VMEM((1, order), jnp.int32),
            pltpu.VMEM((2, shared, loads), F32),
            pltpu.VMEM((2, slots, loads), F32),
            pltpu.VMEM((2, 2 * count, loads), F32),
            pltpu.VMEM((slots, order), BF16),
            pltpu.VMEM((slots, order), BF16),
            pltpu.VMEM((2 * count, slots), BF16),
            dma((7 + order // shared,)),
            dma((wides,)),
            dma((wides,)),
            dma((2, 2, wides)),
            dma((2, 2, wides)),
            dma((OUTER, 2, wides)),
            dma((OUTER, 2, wides)),
            dma((OUTER, 2, narrows)),
            dma((OUTER, 2, narrows)),
        ],
        compiler_params=pltpu.CompilerParams(
            collective_id=0, has_side_effects=True, vmem_limit_bytes=67043328 - 2 * order * loads * 4
        ),
        name="feti",
    )(
        operators[0],
        coarse_inverse,
        modes[0],
        gap[0],
        start_mult[0],
        peer_list.reshape(1, shared),
        partner_row,
        interface_size,
        contact_rows,
    )
    mult, residual = pl.pallas_call(
        flush,
        out_shape=(out, out),
        in_specs=[near] * 2,
        out_specs=(far, far),
        scratch_shapes=[dma((2, 4))],
        compiler_params=pltpu.CompilerParams(vmem_limit_bytes=2**20),
        name="flush",
    )(mult, residual)
    return (mult[None], residual[None])


def solution(mesh):
    everyone = ("groups", "wide", "narrow")
    return jax.shard_map(
        functools.partial(local, mesh.shape["wide"], mesh.shape["narrow"]),
        mesh=mesh,
        in_specs=(
            P(everyone, None, None),
            P(("groups", "wide"), "narrow"),
            P(everyone, None, None),
            P(everyone, None, None),
            P(everyone, None, None),
            P(everyone, None, None),
            P(everyone, None),
            P(everyone),
            P(everyone, None),
        ),
        out_specs=(P(everyone, None, None), P(everyone, None, None)),
        check_vma=False,
    )
```
